32 devices in a mesh: grp: 2 (over x), req: 4 (over z), chan: 4 (over y, core).
Axes of the slice: x: 2, y: 2, z: 4, core: 2. Of those that a mesh axis runs over, the one named last changes fastest.
Arguments:
- tokens: bfloat16 [64, 4096], P(('grp', 'req'), 'chan'), parts along dimension 0, may hold values from -48 to 48
- rec_gain: bfloat16 [4096], P('chan'), may hold values from 0.099609375 to 1.8984375
- rec_in_weight: bfloat16 [2, 4096, 4096], P(None, 'chan', 'req'), may hold values from -0.09375 to 0.09375
- conv_weight: bfloat16 [4, 4096], P(None, 'req'), may hold values from -3 to 3
- conv_bias: bfloat16 [4096], P('req'), may hold values from -3 to 3
- conv_state: bfloat16 [3, 64, 4096], P(None, ('grp', 'chan'), 'req'), parts along dimension 1, may hold values from -5 to 5
- gate_weight: bfloat16 [2, 16, 256, 256], P(None, 'req'), may hold values from -0.375 to 0.375
- gate_bias: bfloat16 [2, 4096], P(None, 'req'), may hold values from -4 to 4
- lru_param: float32 [4096], P('req'), may hold values from -6 to -2
- lru_state: float32 [64, 4096], P(('grp', 'chan'), 'req'), parts along dimension 0, may hold values from -5 to 5
- rec_out_weight: bfloat16 [4096, 4096], P('req', 'chan'), may hold values from -0.09375 to 0.09375
- attn_gain: bfloat16 [4096], P('chan'), may hold values from 0.099609375 to 1.8984375
- query_weight: bfloat16 [4096, 4096], P('chan', 'req'), may hold values from -0.09375 to 0.09375
- kv_weight: bfloat16 [4096, 512], P('chan'), may hold values from -0.09375 to 0.09375
- key_cache: bfloat16 [64, 2048, 256], P(('grp', 'req', 'chan')), parts along dimension 0, may hold values from -400 to 400, as said below
- value_cache: bfloat16 [64, 2048, 256], P(('grp', 'req', 'chan')), parts along dimension 0, may hold values from -5 to 5
- lengths: int32 [64], P(('grp', 'req', 'chan')), parts along dimension 0, may hold values from 1 to 2047, as said below
- write_slots: int32 [64], P(('grp', 'req', 'chan')), parts along dimension 0, may hold values from 0 to 2047, as said below
- attn_out_weight: bfloat16 [4096, 4096], P('req', 'chan'), may hold values from -0.09375 to 0.09375
- mlp_gain: bfloat16 [4096], P('chan'), may hold values from 0.099609375 to 1.8984375
- mlp_in_weight: bfloat16 [2, 4096, 12288], P(None, 'chan', 'req'), may hold values from -0.09375 to 0.09375
- mlp_out_weight: bfloat16 [12288, 4096], P('req', 'chan'), may hold values from -0.0546875 to 0.0546875
Outputs:
- out_tokens: bfloat16 [64, 4096], P(('grp', 'req'), 'chan'), parts along dimension 0
- new_state: float32 [64, 4096], P(('grp', 'chan'), 'req'), parts along dimension 0
- new_entries: bfloat16 [64, 512], P(('grp', 'req', 'chan')), parts along dimension 0
The draws below stay inside these ranges and needn't reach their ends.
There are 2 independent parts, one for each index of `grp`. The reference program is written for one: setup_inputs(seed, part) draws one part's arguments, and reference() takes and returns one part's arrays. A program takes and returns all parts, laid end to end along the dimension named above; an argument that names none is the same for every part. Nothing has to cross between parts.
Inputs may be any that keep to these rules, and one draw needn't show every extreme that they name: `key_cache`: keys as stored, already rotated. `lengths`: earlier tokens of a request that its cache holds. `write_slots`: slot that the new token overwrites; the used slots are the lengths entries just before it, cyclically.
All inputs are finite; a program needn't handle non-finite values.
Results may differ from the reference program's by a relative error of at most 0.011.
Values may be sent and summed in bfloat16 or wider, within the bound.
No kernel may reach another device: no remote copies, remote signals or barrier semaphores. Data moves between devices by JAX's collectives and lax.ppermute only.
A program may use at most 128 MiB of HBM per device.

```python
import math
import jax
import jax.numpy as jnp
from jax import lax

D = 4096
HEADS = 16
HEAD_DIM = 256
FF = 12288
WINDOW = 2048
CONV = 4
LRU = 4096
REQUESTS = 32


def draw_tokens(key, part):
    keys = jax.random.split(jax.random.fold_in(key, 11), 3)
    columns = jnp.arange(D, dtype=jnp.float32) / D - 0.5
    row_scale = jnp.exp(jax.random.uniform(keys[1], (REQUESTS, 1), jnp.float32, math.log(0.3), math.log(3.0)))
    col_scale = jnp.exp(jax.random.uniform(keys[2], (1, D), jnp.float32, math.log(0.3), math.log(3.0)))
    values = jax.random.truncated_normal(keys[0], -3.0, 3.0, (REQUESTS, D), jnp.float32)
    rise = 3.0 ** columns
    result = values * row_scale * col_scale * rise[None, :]
    return jnp.clip(result, -48.0, 48.0).astype(jnp.bfloat16)


def draw_key_cache(key, part):
    keys = jax.random.split(jax.random.fold_in(key, 23), 1)
    base = jax.random.truncated_normal(keys[0], -4.0, 4.0, (REQUESTS, WINDOW, HEAD_DIM), jnp.float32)
    return jnp.clip(base, -400.0, 400.0).astype(jnp.bfloat16)


def draw_lengths(key, part):
    keys = jax.random.split(jax.random.fold_in(key, 37), 3)
    values = jax.random.randint(keys[0], (REQUESTS,), 1, WINDOW)
    first = jax.random.randint(keys[1], (), 0, REQUESTS)
    second = (first + 1 + jax.random.randint(keys[2], (), 0, REQUESTS - 1)) % REQUESTS
    return values.at[first].set(WINDOW - 1).at[second].set(1).astype(jnp.int32)


def draw_write_slots(key, part):
    keys = jax.random.split(jax.random.fold_in(key, 41), 3)
    values = jax.random.randint(keys[0], (REQUESTS,), 0, WINDOW)
    first = jax.random.randint(keys[1], (), 0, REQUESTS)
    second = (first + 1 + jax.random.randint(keys[2], (), 0, REQUESTS - 1)) % REQUESTS
    return values.at[first].set(WINDOW - 1).at[second].set(0).astype(jnp.int32)


def steps_of(own_key, shape, cuts, smallest, top_value):
    level = 1.0
    for dim, shards_of in cuts:
        heights = jax.random.uniform(jax.random.fold_in(jax.random.fold_in(own_key, 6), dim), (shards_of,), jnp.float32, smallest / len(cuts), top_value / len(cuts))
        level = level * jnp.repeat(jnp.exp(heights), shape[dim] // shards_of).reshape((-1,) + (1,) * (len(shape) - 1 - dim))
    return level


def normal_values(key, dims, scale, bound, shards=(), kind=jnp.bfloat16):
    level = steps_of(key, dims, shards, -0.22, 0.18) if shards else 1.0
    entries = jax.random.normal(key, dims, jnp.float32) * scale * level
    return jnp.minimum(jnp.maximum(entries, -bound), bound).astype(kind)


def setup_inputs(seed: int = 0, part: int = 0) -> dict:
    key_of = jax.random.split(jax.random.key(seed), 23)
    part_keys = jax.random.split(jax.random.fold_in(key_of[22], part), 23)
    tokens = draw_tokens(jax.random.fold_in(jax.random.fold_in(key_of[22], part), 71), part)
    rec_gain = jnp.clip(1.0 + 0.18 * jax.random.normal(key_of[1], (D,), jnp.float32), 0.099609375, 1.8984375).astype(jnp.bfloat16)
    rec_in_weight = normal_values(key_of[2], (2, D, LRU), D ** -0.5, 0.09375, ((1, 4), (2, 4)))
    conv_weight = normal_values(key_of[3], (CONV, LRU), CONV ** -0.5, 3.0, ((1, 4),))
    conv_bias = normal_values(key_of[4], (LRU,), 0.5, 3.0, ((0, 4),))
    conv_state = normal_values(part_keys[5], (CONV - 1, REQUESTS, LRU), 1.0, 5.0, ((1, 4), (2, 4)))
    gate_weight = normal_values(key_of[6], (2, HEADS, HEAD_DIM, HEAD_DIM), HEAD_DIM ** -0.5, 0.375, ((1, 4),))
    gate_bias = normal_values(key_of[7], (2, LRU), 1.0, 4.0, ((1, 4),))
    lru_param = jnp.clip(-6.0 + 4.0 * jax.random.uniform(key_of[8], (LRU,), jnp.float32) ** steps_of(key_of[8], (LRU,), ((0, 4),), -0.2, 0.2), -6.0, -2.0)
    lru_state = normal_values(part_keys[9], (REQUESTS, LRU), 1.0, 5.0, ((0, 4), (1, 4)), jnp.float32)
    rec_out_weight = normal_values(key_of[10], (LRU, D), LRU ** -0.5, 0.09375, ((0, 4), (1, 4)))
    attn_gain = jnp.clip(1.0 + 0.18 * jax.random.normal(key_of[11], (D,), jnp.float32), 0.099609375, 1.8984375).astype(jnp.bfloat16)
    query_weight = normal_values(key_of[12], (D, HEADS * HEAD_DIM), D ** -0.5, 0.09375, ((0, 4), (1, 4)))
    kv_weight = normal_values(key_of[13], (D, 2 * HEAD_DIM), D ** -0.5, 0.09375, ((0, 4),))
    key_cache = draw_key_cache(jax.random.fold_in(jax.random.fold_in(key_of[22], part), 71), part)
    value_cache = normal_values(part_keys[15], (REQUESTS, WINDOW, HEAD_DIM), 1.0, 5.0, ((0, 16),))
    lengths = draw_lengths(jax.random.fold_in(jax.random.fold_in(key_of[22], part), 71), part)
    write_slots = draw_write_slots(jax.random.fold_in(jax.random.fold_in(key_of[22], part), 71), part)
    attn_out_weight = normal_values(key_of[18], (HEADS * HEAD_DIM, D), (HEADS * HEAD_DIM) ** -0.5, 0.09375, ((0, 4), (1, 4)))
    mlp_gain = jnp.clip(1.0 + 0.18 * jax.random.normal(key_of[19], (D,), jnp.float32), 0.099609375, 1.8984375).astype(jnp.bfloat16)
    mlp_in_weight = normal_values(key_of[20], (2, D, FF), D ** -0.5, 0.09375, ((1, 4), (2, 4)))
    mlp_out_weight = normal_values(key_of[21], (FF, D), FF ** -0.5, 0.0546875, ((0, 4), (1, 4)))
    return dict(tokens=tokens, rec_gain=rec_gain, rec_in_weight=rec_in_weight, conv_weight=conv_weight, conv_bias=conv_bias, conv_state=conv_state, gate_weight=gate_weight, gate_bias=gate_bias, lru_param=lru_param, lru_state=lru_state, rec_out_weight=rec_out_weight, attn_gain=attn_gain, query_weight=query_weight, kv_weight=kv_weight, key_cache=key_cache, value_cache=value_cache, lengths=lengths, write_slots=write_slots, attn_out_weight=attn_out_weight, mlp_gain=mlp_gain, mlp_in_weight=mlp_in_weight, mlp_out_weight=mlp_out_weight)


EPS = 1e-06

def rms_scale(stream, gain):
    mean_sq = lax.optimization_barrier(jnp.mean(stream * stream, axis=-1, keepdims=True))
    return (stream * lax.rsqrt(mean_sq + EPS) * gain.astype(jnp.float32)).astype(jnp.bfloat16)

def rotate(vector, position):
    half = vector.shape[-1] // 2
    freq = 10000.0 ** (-jnp.arange(half, dtype=jnp.float32) / half)
    angle = position[..., None] * freq
    cosine = jnp.cos(angle)
    sine = jnp.sin(angle)
    first = vector[..., :half]
    second = vector[..., half:]
    return jnp.concatenate([first * cosine - second * sine, second * cosine + first * sine], axis=-1)

def reference(tokens, rec_gain, rec_in_weight, conv_weight, conv_bias, conv_state, gate_weight, gate_bias, lru_param, lru_state, rec_out_weight, attn_gain, query_weight, kv_weight, key_cache, value_cache, lengths, write_slots, attn_out_weight, mlp_gain, mlp_in_weight, mlp_out_weight):
    stream = tokens.astype(jnp.float32)
    normed = rms_scale(stream, rec_gain)
    branch_x = jnp.dot(normed, rec_in_weight[0], preferred_element_type=jnp.float32)
    branch_y = jnp.dot(normed, rec_in_weight[1], preferred_element_type=jnp.float32)
    taps = conv_weight.astype(jnp.float32)
    convolved = taps[0] * branch_x + conv_bias.astype(jnp.float32)
    for offset in range(CONV - 1):
        convolved = convolved + taps[offset + 1] * conv_state[offset].astype(jnp.float32)
    conv_low = convolved.astype(jnp.bfloat16).astype(jnp.float32).reshape(REQUESTS, HEADS, HEAD_DIM)
    gates = jnp.einsum('rhi,ghio->grho', conv_low, gate_weight.astype(jnp.float32)).reshape(2, REQUESTS, LRU)
    gates = gates + gate_bias.astype(jnp.float32)[:, None, :]
    log_decay = -8.0 * jax.nn.sigmoid(gates[0]) * jax.nn.softplus(lru_param)[None, :]
    new_state = jnp.exp(log_decay) * lru_state + jnp.sqrt(1.0 - jnp.exp(2.0 * log_decay)) * (jax.nn.sigmoid(gates[1]) * convolved)
    mixed = (new_state * jax.nn.gelu(branch_y, approximate=True)).astype(jnp.bfloat16)
    stream = stream + jnp.dot(mixed, rec_out_weight, preferred_element_type=jnp.float32)
    normed = rms_scale(stream, attn_gain)
    query = jnp.dot(normed, query_weight, preferred_element_type=jnp.float32).astype(jnp.bfloat16)
    key_value = jnp.dot(normed, kv_weight, preferred_element_type=jnp.float32)
    position = lengths.astype(jnp.float32)
    query_rot = rotate(query.astype(jnp.float32).reshape(REQUESTS, HEADS, HEAD_DIM), position[:, None])
    query_rot = (query_rot * HEAD_DIM ** (-0.5)).astype(jnp.bfloat16)
    key_new = rotate(key_value[:, :HEAD_DIM], position).astype(jnp.bfloat16)
    value_new = key_value[:, HEAD_DIM:].astype(jnp.bfloat16)

    def attend(item):
        query_one, keys_one, values_one, key_one, value_one, length_one, slot_one = item
        scores = jnp.einsum('hd,jd->hj', query_one.astype(jnp.float32), keys_one.astype(jnp.float32))
        self_score = jnp.einsum('hd,d->h', query_one.astype(jnp.float32), key_one.astype(jnp.float32))
        slot_age = (slot_one - jnp.arange(WINDOW, dtype=jnp.int32)) % WINDOW
        is_valid = (slot_age >= 1) & (slot_age <= length_one)
        masked = jnp.where(is_valid[None, :], scores, -1e+30)
        row_top = jnp.maximum(lax.optimization_barrier(jnp.max(masked, axis=1)), self_score)
        weights = jnp.exp(masked - row_top[:, None])
        self_weight = jnp.exp(self_score - row_top)
        row_total = lax.optimization_barrier(jnp.sum(weights, axis=1)) + self_weight
        weights_low = (weights / row_total[:, None]).astype(jnp.bfloat16)
        self_low = (self_weight / row_total).astype(jnp.bfloat16)
        result = jnp.einsum('hj,jd->hd', weights_low.astype(jnp.float32), values_one.astype(jnp.float32))
        result = result + self_low.astype(jnp.float32)[:, None] * value_one.astype(jnp.float32)[None, :]
        return result.astype(jnp.bfloat16)
    attended = lax.map(attend, (query_rot, key_cache, value_cache, key_new, value_new, lengths, write_slots))
    attended = attended.reshape(REQUESTS, HEADS * HEAD_DIM)
    stream = stream + jnp.dot(attended, attn_out_weight, preferred_element_type=jnp.float32)
    normed = rms_scale(stream, mlp_gain)
    gate_part = jnp.dot(normed, mlp_in_weight[0], preferred_element_type=jnp.float32)
    up_part = jnp.dot(normed, mlp_in_weight[1], preferred_element_type=jnp.float32)
    hidden = (jax.nn.gelu(gate_part, approximate=True) * up_part).astype(jnp.bfloat16)
    stream = stream + jnp.dot(hidden, mlp_out_weight, preferred_element_type=jnp.float32)
    new_entries = jnp.concatenate([key_new, value_new], axis=1)
    return (stream.astype(jnp.bfloat16), new_state, new_entries)
```

```python
import jax
import jax.numpy as jnp
from jax import lax
from jax.sharding import PartitionSpec as P

EPS = 1e-06
F32 = jnp.float32
BF16 = jnp.bfloat16
LANES = 128


def swap(value, axis, mask):
    return lax.ppermute(value, axis, [(i, i ^ mask) for i in range(lax.axis_size(axis))])


def in_order(blocks, index):
    bit = 1
    while bit < len(blocks):
        flip = (index & bit) != 0
        blocks = [jnp.where(flip, blocks[b ^ bit], blocks[b]) for b in range(len(blocks))]
        bit *= 2
    return blocks


def gather_rows(value, axis):
    blocks = [value] + [swap(value, axis, m) for m in range(1, lax.axis_size(axis))]
    return jnp.concatenate(in_order(blocks, lax.axis_index(axis)), axis=0)


def exchange_sum(part, axis, masks):
    low = part.astype(BF16)
    total = part
    for m in masks:
        total = total + swap(low, axis, m).astype(F32)
    return total


def square_lanes(squares):
    high = lax.reduce_precision(squares, 8, 7)
    low = squares - high
    half = (squares.shape[0], LANES // 2)
    return jnp.concatenate(
        [jnp.broadcast_to(high[:, None], half), jnp.broadcast_to(low[:, None], half)], axis=1
    )


def factor_of(lanes, features):
    squares = lanes[..., 0] + lanes[..., LANES // 2]
    return lax.rsqrt(squares / features + EPS)


def scaled(stream, gain):
    return (stream * gain.astype(F32)).astype(BF16), jnp.sum(stream * stream, axis=1)


def rotate(vector, position):
    half = vector.shape[-1] // 2
    freq = 10000.0 ** (-jnp.arange(half, dtype=F32) / half)
    angle = position[..., None] * freq
    cosine = jnp.cos(angle)
    sine = jnp.sin(angle)
    first = vector[..., :half]
    second = vector[..., half:]
    return jnp.concatenate(
        [first * cosine - second * sine, second * cosine + first * sine], axis=-1
    )


def dot(a, b):
    return jnp.dot(a, b, preferred_element_type=F32)


def per_device(
    tokens,
    rec_gain,
    rec_in_weight,
    conv_weight,
    conv_bias,
    conv_state,
    gate_weight,
    gate_bias,
    lru_param,
    lru_state,
    rec_out_weight,
    attn_gain,
    query_weight,
    kv_weight,
    key_cache,
    value_cache,
    lengths,
    write_slots,
    attn_out_weight,
    mlp_gain,
    mlp_in_weight,
    mlp_out_weight,
):
    nr = lax.axis_size("req")
    nc = lax.axis_size("chan")
    row = lax.axis_index("req")
    col = lax.axis_index("chan")
    features = tokens.shape[1] * nc
    req_masks = range(1, nr)
    chan_masks = range(1, nc)
    tokens_all = gather_rows(tokens, "req").astype(F32)
    rows_all = tokens_all.shape[0]
    normed, squares = scaled(tokens_all, rec_gain)
    part = jnp.concatenate(
        [dot(normed, rec_in_weight[0]), dot(normed, rec_in_weight[1]), square_lanes(squares)],
        axis=1,
    ).reshape(nc, rows_all // nc, -1)
    total = lax.dynamic_index_in_dim(part, col, 0, keepdims=False)
    low = part.astype(BF16)
    for m in chan_masks:
        total = total + swap(
            lax.dynamic_index_in_dim(low, col ^ m, 0, keepdims=False), "chan", m
        ).astype(F32)
    lru_here = lru_state.shape[1]
    factor = factor_of(total[:, 2 * lru_here :], features)[:, None]
    branch_x = total[:, :lru_here] * factor
    branch_y = total[:, lru_here : 2 * lru_here] * factor
    taps = conv_weight.astype(F32)
    convolved = taps[0] * branch_x + conv_bias.astype(F32)
    for offset in range(conv_state.shape[0]):
        convolved = convolved + taps[offset + 1] * conv_state[offset].astype(F32)
    rows_here = convolved.shape[0]
    blocks_here = gate_weight.shape[1]
    conv_low = convolved.astype(BF16).reshape(rows_here, blocks_here, -1)
    gates = jnp.einsum("rhi,ghio->grho", conv_low, gate_weight, preferred_element_type=F32)
    gates = gates.reshape(2, rows_here, lru_here) + gate_bias.astype(F32)[:, None, :]
    log_decay = -8.0 * jax.nn.sigmoid(gates[0]) * jax.nn.softplus(lru_param)[None, :]
    new_state = jnp.exp(log_decay) * lru_state + jnp.sqrt(1.0 - jnp.exp(2.0 * log_decay)) * (
        jax.nn.sigmoid(gates[1]) * convolved
    )
    mixed = (new_state * jax.nn.gelu(branch_y, approximate=True)).astype(BF16)
    rec_return = dot(gather_rows(mixed, "chan"), rec_out_weight)
    stream = tokens_all + exchange_sum(rec_return, "req", req_masks)
    normed, squares = scaled(stream, attn_gain)
    kv_here = kv_weight.shape[1] // nr
    kv_slice = lax.dynamic_slice_in_dim(kv_weight, row * kv_here, kv_here, 1)
    owner_rows = rows_all // (nr * nc)
    heads_here = query_weight.shape[1]
    sent = jnp.concatenate(
        [dot(normed, query_weight), dot(normed, kv_slice), square_lanes(squares)], axis=1
    ).astype(BF16)
    arrived = lax.all_to_all(
        sent.reshape(nr * nc, owner_rows, -1),
        ("req", "chan"),
        split_axis=0,
        concat_axis=0,
        tiled=True,
    )
    summed = jnp.sum(arrived.astype(F32).reshape(nr, nc, owner_rows, -1), axis=1)
    factor = factor_of(summed[0, :, heads_here + kv_here :], features)[None, :, None]
    query = (summed[:, :, :heads_here] * factor).astype(BF16)
    query = query.transpose(1, 0, 2).reshape(owner_rows, nr * heads_here)
    key_value = (summed[:, :, heads_here : heads_here + kv_here] * factor).transpose(1, 0, 2)
    key_value = key_value.reshape(owner_rows, nr * kv_here)
    head_dim = key_value.shape[1] // 2
    position = lengths.astype(F32)
    query_rot = rotate(query.astype(F32).reshape(owner_rows, -1, head_dim), position[:, None])
    query_rot = (query_rot * head_dim ** (-0.5)).astype(BF16)
    key_new = rotate(key_value[:, :head_dim], position).astype(BF16)
    value_new = key_value[:, head_dim:].astype(BF16)
    scores = jnp.einsum("rhd,rjd->rhj", query_rot, key_cache, preferred_element_type=F32)
    self_score = jnp.einsum("rhd,rd->rh", query_rot, key_new, preferred_element_type=F32)
    window = key_cache.shape[1]
    slot_age = (write_slots[:, None] - jnp.arange(window, dtype=jnp.int32)[None, :]) % window
    is_valid = (slot_age >= 1) & (slot_age <= lengths[:, None])
    masked = jnp.where(is_valid[:, None, :], scores, -1e30)
    row_top = jnp.maximum(jnp.max(masked, axis=2), self_score)
    weights = jnp.exp(masked - row_top[..., None])
    self_weight = jnp.exp(self_score - row_top)
    row_total = jnp.sum(weights, axis=2) + self_weight
    weights_low = (weights / row_total[..., None]).astype(BF16)
    self_low = (self_weight / row_total).astype(BF16)
    attended = jnp.einsum("rhj,rjd->rhd", weights_low, value_cache, preferred_element_type=F32)
    attended = attended + self_low.astype(F32)[..., None] * value_new.astype(F32)[:, None, :]
    attended = attended.astype(BF16).reshape(owner_rows, nr, heads_here).transpose(1, 0, 2)
    attended = jnp.broadcast_to(attended[:, None], (nr, nc, owner_rows, heads_here))
    attended = lax.all_to_all(
        attended.reshape(nr * nc, owner_rows, heads_here),
        ("req", "chan"),
        split_axis=0,
        concat_axis=0,
        tiled=True,
    ).reshape(rows_all, heads_here)
    stream = stream + exchange_sum(dot(attended, attn_out_weight), "req", req_masks)
    normed, squares = scaled(stream, mlp_gain)
    cores = 2 if nc % 2 == 0 else 1
    hidden_here = mlp_in_weight.shape[2] // cores
    core = col % cores
    gate_part = dot(normed, mlp_in_weight[0]).reshape(rows_all, cores, hidden_here)
    up_part = dot(normed, mlp_in_weight[1]).reshape(rows_all, cores, hidden_here)
    lanes = square_lanes(squares)

    def half(index):
        return jnp.concatenate(
            [
                lax.dynamic_index_in_dim(gate_part, index, 1, keepdims=False),
                lax.dynamic_index_in_dim(up_part, index, 1, keepdims=False),
                lanes,
            ],
            axis=1,
        )

    total = half(core)
    if cores == 2:
        total = total + swap(half(core ^ 1).astype(BF16), "chan", 1).astype(F32)
    lanes = square_lanes(total[:, 2 * hidden_here] + total[:, 2 * hidden_here + LANES // 2])
    total = jnp.concatenate([total[:, : 2 * hidden_here], lanes], axis=1)
    total = exchange_sum(total, "chan", range(cores, nc, cores))
    factor = factor_of(total[:, 2 * hidden_here :], features)[:, None]
    hidden = jax.nn.gelu(total[:, :hidden_here] * factor, approximate=True) * (
        total[:, hidden_here : 2 * hidden_here] * factor
    )
    hidden = hidden.astype(BF16)
    if cores == 2:
        hidden = jnp.concatenate(in_order([hidden, swap(hidden, "chan", 1)], core), axis=1)
    down = dot(hidden, mlp_out_weight).reshape(nr, rows_all // nr, -1)
    down_low = down.astype(BF16)
    result = lax.dynamic_index_in_dim(stream.reshape(down.shape), row, 0, keepdims=False)
    result = result + lax.dynamic_index_in_dim(down, row, 0, keepdims=False)
    for m in req_masks:
        result = result + swap(
            lax.dynamic_index_in_dim(down_low, row ^ m, 0, keepdims=False), "req", m
        ).astype(F32)
    new_entries = jnp.concatenate([key_new, value_new], axis=1)
    return (result.astype(BF16), new_state, new_entries)


def solution(mesh):
    return jax.shard_map(
        per_device,
        mesh=mesh,
        in_specs=(
            P(("grp", "req"), "chan"),
            P("chan"),
            P(None, "chan", "req"),
            P(None, "req"),
            P("req"),
            P(None, ("grp", "chan"), "req"),
            P(None, "req", None, None),
            P(None, "req"),
            P("req"),
            P(("grp", "chan"), "req"),
            P("req", "chan"),
            P("chan"),
            P("chan", "req"),
            P("chan", None),
            P(("grp", "req", "chan"), None, None),
            P(("grp", "req", "chan"), None, None),
            P(("grp", "req", "chan")),
            P(("grp", "req", "chan")),
            P("req", "chan"),
            P("chan"),
            P(None, "chan", "req"),
            P("req", "chan"),
        ),
        out_specs=(
            P(("grp", "req"), "chan"),
            P(("grp", "chan"), "req"),
            P(("grp", "req", "chan"), None),
        ),
        check_vma=False,
    )
```

```python
import functools

import jax
import jax.numpy as jnp
from jax import lax
from jax.experimental import pallas as pl
from jax.experimental.pallas import tpu as pltpu
from jax.sharding import PartitionSpec as P

EPS = 1e-06
F32 = jnp.float32
BF16 = jnp.bfloat16
LANES = 128
MIB = 1024 * 1024


def swap(value, axis, mask):
    return lax.ppermute(value, axis, [(i, i ^ mask) for i in range(lax.axis_size(axis))])


def on_chip(weight):
    return pltpu.with_memory_space_constraint(weight, pltpu.VMEM)


def shape(dims, dtype):
    return jax.ShapeDtypeStruct(dims, dtype)


def call(kernel, name, outs, scalars, arrays, scratch=(), grant=6):
    work = sum(a.size * a.dtype.itemsize for a in arrays)
    return pl.pallas_call(
        kernel,
        out_shape=outs,
        in_specs=[pl.BlockSpec(memory_space=pltpu.SMEM)] * len(scalars)
        + [pl.BlockSpec(memory_space=pltpu.VMEM)] * len(arrays),
        out_specs=[pl.BlockSpec(memory_space=pltpu.VMEM)] * len(outs),
        scratch_shapes=list(scratch),
        compiler_params=pltpu.CompilerParams(vmem_limit_bytes=grant * MIB),
        cost_estimate=pl.CostEstimate(flops=32 * work, bytes_accessed=work, transcendentals=0),
        name=name,
    )(*scalars, *arrays)


def dot(a, b):
    return jnp.dot(a, b, preferred_element_type=F32)


def product(normed, weight, write, width=512):
    columns = weight.shape[-1]
    step = width if columns % width == 0 else columns
    for at in range(0, columns, step):
        write(at, step, dot(normed, weight[:, at : at + step]))


def square_lanes(squares):
    high = squares.astype(BF16).astype(F32)
    low = squares - high
    lane = lax.broadcasted_iota(jnp.int32, (squares.shape[0], LANES), 1)
    return jnp.where(lane < LANES // 2, high, low)


def factor_of(lanes, features):
    squares = lanes[:, :1] + lanes[:, LANES // 2 : LANES // 2 + 1]
    return lax.rsqrt(squares / features + EPS)


def sum_squares(stream):
    return jnp.sum(stream * stream, axis=1, keepdims=True)


def gelu(v):
    return 0.5 * v * (1.0 + jnp.tanh(0.7978845608028654 * (v + 0.044715 * (v * v * v))))


def sigmoid(v):
    return 1.0 / (1.0 + jnp.exp(-v))


def rows_of(block, size):
    return pl.ds(pl.multiple_of(block * size, size), size)


def rec_in_kernel(nr, nc, at_ref, *refs):
    blocks, refs = refs[:nr], refs[nr:]
    gain, weight, tokens_all, keep = refs[:4]
    lows, (stream, part) = refs[4 : 3 + nc], refs[3 + nc :]
    row, col = at_ref[0], at_ref[1]
    size = blocks[0].shape[0]
    for m in range(nr):
        stream[rows_of(row ^ m, size), :] = blocks[m][...].astype(F32)
    value = stream[...]
    tokens_all[...] = value.astype(BF16)
    here = weight.shape[2]
    part[:, 2 * here :] = square_lanes(sum_squares(value))
    normed = (value * gain[...].astype(F32)).astype(BF16)
    for g in range(2):

        def write(at, step, result):
            part[:, g * here + at : g * here + at + step] = result

        product(normed, weight.at[g], write)
    size = keep.shape[0]
    for m in range(1, nc):
        lows[m - 1][...] = part[rows_of(col ^ m, size), :].astype(BF16)
    keep[...] = part[rows_of(col, size), :]


def recurrent_kernel(nc, features, *refs):
    keep, lows, refs = refs[0], refs[1:nc], refs[nc:]
    taps, bias, conv_state, gate_weight, gate_bias, lru_param, lru_state, state_ref, mixed_ref = refs
    here = lru_state.shape[1]
    total = keep[...]
    for low in lows:
        total = total + low[...].astype(F32)
    factor = factor_of(total[:, 2 * here :], features)
    convolved = taps[0:1, :].astype(F32) * (total[:, :here] * factor) + bias[...].astype(F32)
    for offset in range(conv_state.shape[0]):
        convolved = convolved + taps[offset + 1 : offset + 2, :].astype(F32) * conv_state[
            offset
        ].astype(F32)
    conv_low = convolved.astype(BF16)
    size = gate_weight.shape[2]
    for h in range(gate_weight.shape[1]):
        cut = slice(h * size, (h + 1) * size)
        decay_gate = dot(conv_low[:, cut], gate_weight[0, h]) + gate_bias[0:1, cut].astype(F32)
        input_gate = dot(conv_low[:, cut], gate_weight[1, h]) + gate_bias[1:2, cut].astype(F32)
        softplus = jnp.log(1.0 + jnp.exp(lru_param[:, cut]))
        log_decay = -8.0 * sigmoid(decay_gate) * softplus
        state = jnp.exp(log_decay) * lru_state[:, cut] + jnp.sqrt(
            1.0 - jnp.exp(2.0 * log_decay)
        ) * (sigmoid(input_gate) * convolved[:, cut])
        state_ref[:, cut] = state
        branch_y = total[:, here + h * size : here + (h + 1) * size] * factor
        mixed_ref[:, cut] = (state * gelu(branch_y)).astype(BF16)


def rec_out_kernel(nc, at_ref, *refs):
    blocks, (weight, low, mixed) = refs[:nc], refs[nc:]
    size = blocks[0].shape[0]
    for m in range(nc):
        mixed[rows_of(at_ref[1] ^ m, size), :] = blocks[m][...].astype(F32)

    def write(at, step, result):
        low[:, at : at + step] = result.astype(BF16)

    product(mixed[...].astype(BF16), weight, write)


def query_kernel(nr, *refs):
    stream, lows, refs = refs[0], refs[1 : 1 + nr], refs[1 + nr :]
    gain, query_weight, kv_slice, stream_out, sent, part = refs
    value = stream[...].astype(F32)
    for low in lows:
        value = value + low[...].astype(F32)
    stream_out[...] = value
    heads = query_weight.shape[1]
    part[:, heads : heads + LANES] = square_lanes(sum_squares(value))
    normed = (value * gain[...].astype(F32)).astype(BF16)

    def write(at, step, result):
        part[:, at : at + step] = result

    product(normed, query_weight, write)
    part[:, heads + LANES :] = dot(normed, kv_slice[...])
    size = sent.shape[1]
    for block in range(sent.shape[0]):
        sent[block] = part[block * size : (block + 1) * size, :].astype(BF16)


def turn(v, cosine, sine):
    half = cosine.shape[1]
    first, second = v[:, :half], v[:, half:]
    return jnp.concatenate(
        [first * cosine - second * sine, second * cosine + first * sine], axis=1
    )


def attention_kernel(nr, nc, features, lengths, slots, *refs):
    arrived, cosine_ref, sine_ref, keys, values, sent, entries, query, attended, kv = refs
    owners, window, head_dim = keys.shape
    cosine, sine = cosine_ref[...], sine_ref[...]
    heads_here = sent.shape[2]
    group = heads_here // head_dim
    kv_here = kv.shape[1] // nr
    scale = head_dim ** (-0.5)
    factor = None
    for r in range(nr):
        total = jnp.sum(arrived[r * nc : (r + 1) * nc].astype(F32), axis=0)
        if factor is None:
            factor = factor_of(total[:, heads_here : heads_here + LANES], features)
        kv[:, r * kv_here : (r + 1) * kv_here] = total[:, heads_here + LANES :] * factor
        low = (total[:, :heads_here] * factor).astype(BF16).astype(F32)
        for h in range(group):
            turned = turn(low[:, h * head_dim : (h + 1) * head_dim], cosine, sine) * scale
            for b in range(owners):
                query[b, r * group + h : r * group + h + 1, :] = turned[b : b + 1, :]
    key_new = turn(kv[:, :head_dim], cosine, sine).astype(BF16)
    value_new = kv[:, head_dim:].astype(BF16)
    entries[:, :head_dim] = key_new
    entries[:, head_dim:] = value_new
    slot_index = lax.broadcasted_iota(jnp.int32, (1, window), 1)
    for b in range(owners):
        q = query[b].astype(BF16)
        scores = lax.dot_general(
            q, keys[b], (((1,), (1,)), ((), ())), preferred_element_type=F32
        )
        self_score = jnp.sum(
            q.astype(F32) * key_new[b : b + 1, :].astype(F32), axis=1, keepdims=True
        )
        age = slots[b] - slot_index
        age = jnp.where(age < 0, age + window, age)
        valid = (age >= 1) & (age <= lengths[b])
        masked = jnp.where(valid, scores, -1e30)
        top = jnp.maximum(jnp.max(masked, axis=1, keepdims=True), self_score)
        weights = jnp.exp(masked - top)
        self_weight = jnp.exp(self_score - top)
        total = jnp.sum(weights, axis=1, keepdims=True) + self_weight
        result = dot((weights / total).astype(BF16), values[b])
        self_low = (self_weight / total).astype(BF16).astype(F32)
        result = result + self_low * value_new[b : b + 1, :].astype(F32)
        for h in range(nr * group):
            attended[b : b + 1, h * head_dim : (h + 1) * head_dim] = result[h : h + 1, :]
    for r in range(nr):
        low = attended[:, r * heads_here : (r + 1) * heads_here].astype(BF16)
        for c in range(nc):
            sent[r * nc + c] = low


def attn_out_kernel(arrived, weight, low, rows):
    size = arrived.shape[1]
    for block in range(arrived.shape[0]):
        rows[block * size : (block + 1) * size, :] = arrived[block].astype(F32)

    def write(at, step, result):
        low[:, at : at + step] = result.astype(BF16)

    product(rows[...].astype(BF16), weight, write)


def mlp_in_kernel(nr, cores, at_ref, *refs):
    stream, lows, refs = refs[0], refs[1 : 1 + nr], refs[1 + nr :]
    gain, weight, stream_out, keep = refs[:4]
    value = stream[...]
    for low in lows:
        value = value + low[...].astype(F32)
    stream_out[...] = value
    normed = (value * gain[...].astype(F32)).astype(BF16)
    lanes = square_lanes(sum_squares(value))
    here = weight.shape[2] // cores
    core = at_ref[1] % cores
    for m in reversed(range(cores)):
        out = refs[3 + m]
        out[:, 2 * here :] = lanes.astype(out.dtype)
        start = (core ^ m) * here
        step = 512 if here % 512 == 0 else here
        for g in range(2):
            for at in range(0, here, step):
                cut = pl.ds(pl.multiple_of(start + at, LANES), step)
                out[:, g * here + at : g * here + at + step] = dot(
                    normed, weight[g, :, cut]
                ).astype(out.dtype)


def pair_kernel(keep, arrived, low):
    wide = low.shape[1] - LANES
    total = keep[...] + arrived[...].astype(F32)
    low[:, :wide] = total[:, :wide].astype(BF16)
    squares = total[:, wide : wide + 1] + total[:, wide + LANES // 2 : wide + LANES // 2 + 1]
    low[:, wide:] = square_lanes(squares).astype(BF16)


def hidden_kernel(features, *refs):
    lows, hidden = refs[:-1], refs[-1]
    here = hidden.shape[1]
    total = lows[0][...].astype(F32)
    for low in lows[1:]:
        total = total + low[...].astype(F32)
    factor = factor_of(total[:, 2 * here :], features)
    hidden[...] = (gelu(total[:, :here] * factor) * (total[:, here : 2 * here] * factor)).astype(
        BF16
    )


def mlp_out_kernel(nr, cores, at_ref, *refs):
    hiddens, refs = refs[:cores], refs[cores:]
    stream, weight, keep = refs[:3]
    lows, part = refs[3 : 2 + nr], refs[2 + nr]
    here = hiddens[0].shape[1]
    core, row = at_ref[1] % cores, at_ref[0]
    columns = weight.shape[1]
    step = 512 if columns % 512 == 0 else columns
    for at in range(0, columns, step):
        total = None
        for m in range(cores):
            cut = pl.ds(pl.multiple_of((core ^ m) * here, LANES), here)
            result = dot(hiddens[m][...], weight[cut, at : at + step])
            total = result if total is None else total + result
        part[:, at : at + step] = total
    size = keep.shape[0]
    for m in range(1, nr):
        lows[m - 1][...] = part[rows_of(row ^ m, size), :].astype(BF16)
    own = rows_of(row, size)
    keep[...] = part[own, :] + stream[own, :]


def result_kernel(*refs):
    total = refs[0][...]
    for low in refs[1:-1]:
        total = total + low[...].astype(F32)
    refs[-1][...] = total.astype(BF16)


def per_device(
    tokens,
    rec_gain,
    rec_in_weight,
    conv_weight,
    conv_bias,
    conv_state,
    gate_weight,
    gate_bias,
    lru_param,
    lru_state,
    rec_out_weight,
    attn_gain,
    query_weight,
    kv_weight,
    key_cache,
    value_cache,
    lengths,
    write_slots,
    attn_out_weight,
    mlp_gain,
    mlp_in_weight,
    mlp_out_weight,
):
    nr = lax.axis_size("req")
    nc = lax.axis_size("chan")
    at = jnp.stack([lax.axis_index("req"), lax.axis_index("chan")]).astype(jnp.int32)
    local_rows, local_features = tokens.shape
    rows = local_rows * nr
    features = local_features * nc
    lru_rows, lru_here = lru_state.shape
    blocks = [tokens] + [swap(tokens, "req", m) for m in range(1, nr)]
    wide = 2 * lru_here + LANES
    tokens_all, keep, *lows = call(
        functools.partial(rec_in_kernel, nr, nc),
        "rec_in",
        [shape((rows, local_features), BF16), shape((lru_rows, wide), F32)]
        + [shape((lru_rows, wide), BF16)] * (nc - 1),
        [at],
        blocks + [rec_gain[None, :], on_chip(rec_in_weight)],
        [pltpu.VMEM((rows, local_features), F32), pltpu.VMEM((rows, wide), F32)],
    )
    lows = [swap(low, "chan", m + 1) for m, low in enumerate(lows)]
    new_state, mixed = call(
        functools.partial(recurrent_kernel, nc, features),
        "recurrent",
        [shape((lru_rows, lru_here), F32), shape((lru_rows, lru_here), BF16)],
        [],
        [keep]
        + lows
        + [
            conv_weight,
            conv_bias[None, :],
            conv_state,
            on_chip(gate_weight),
            gate_bias,
            lru_param[None, :],
            lru_state,
        ],
    )
    (low,) = call(
        functools.partial(rec_out_kernel, nc),
        "rec_out",
        [shape((rows, local_features), BF16)],
        [at],
        [mixed] + [swap(mixed, "chan", m) for m in range(1, nc)] + [on_chip(rec_out_weight)],
        [pltpu.VMEM((rows, lru_here), F32)],
    )
    lows = [low] + [swap(low, "req", m) for m in range(1, nr)]
    kv_here = kv_weight.shape[1] // nr
    kv_slice = lax.dynamic_slice_in_dim(kv_weight, at[0] * kv_here, kv_here, 1)
    owners = rows // (nr * nc)
    heads_here = query_weight.shape[1]
    wide = heads_here + LANES + kv_here
    stream, sent = call(
        functools.partial(query_kernel, nr),
        "query",
        [shape((rows, local_features), F32), shape((nr * nc, owners, wide), BF16)],
        [],
        [tokens_all] + lows + [attn_gain[None, :], on_chip(query_weight), kv_slice],
        [pltpu.VMEM((rows, wide), F32)],
    )
    arrived = lax.all_to_all(sent, ("req", "chan"), split_axis=0, concat_axis=0, tiled=True)
    head_dim = key_cache.shape[2]
    freq = 10000.0 ** (-jnp.arange(head_dim // 2, dtype=F32) / (head_dim // 2))
    angle = lengths.astype(F32)[:, None] * freq
    sent, new_entries = call(
        functools.partial(attention_kernel, nr, nc, features),
        "attention",
        [shape((nr * nc, owners, heads_here), BF16), shape((owners, 2 * head_dim), BF16)],
        [lengths, write_slots],
        [arrived, jnp.cos(angle), jnp.sin(angle), on_chip(key_cache), on_chip(value_cache)],
        [
            pltpu.VMEM((owners, nr * heads_here // head_dim, head_dim), F32),
            pltpu.VMEM((owners, nr * heads_here), F32),
            pltpu.VMEM((owners, 2 * head_dim), F32),
        ],
    )
    arrived = lax.all_to_all(sent, ("req", "chan"), split_axis=0, concat_axis=0, tiled=True)
    (low,) = call(
        attn_out_kernel,
        "attn_out",
        [shape((rows, local_features), BF16)],
        [],
        [arrived, on_chip(attn_out_weight)],
        [pltpu.VMEM((rows, heads_here), F32)],
    )
    lows = [low] + [swap(low, "req", m) for m in range(1, nr)]
    cores = 2 if nc % 2 == 0 else 1
    hidden_here = mlp_in_weight.shape[2] // cores
    wide = 2 * hidden_here + LANES
    stream, keep, *lows = call(
        functools.partial(mlp_in_kernel, nr, cores),
        "mlp_in",
        [shape((rows, local_features), F32), shape((rows, wide), F32)]
        + [shape((rows, wide), BF16)] * (cores - 1),
        [at],
        [stream] + lows + [mlp_gain[None, :], on_chip(mlp_in_weight)],
    )
    if cores == 2:
        (low,) = call(
            pair_kernel,
            "pair",
            [shape((rows, wide), BF16)],
            [],
            [keep, swap(lows[0], "chan", 1)],
        )
    else:
        low = keep.astype(BF16)
    (hidden,) = call(
        functools.partial(hidden_kernel, features),
        "hidden",
        [shape((rows, hidden_here), BF16)],
        [],
        [low] + [swap(low, "chan", m) for m in range(cores, nc, cores)],
    )
    keep, *lows = call(
        functools.partial(mlp_out_kernel, nr, cores),
        "mlp_out",
        [shape((local_rows, local_features), F32)]
        + [shape((local_rows, local_features), BF16)] * (nr - 1),
        [at],
        [hidden]
        + [swap(hidden, "chan", m) for m in range(1, cores)]
        + [stream, on_chip(mlp_out_weight)],
        [pltpu.VMEM((rows, local_features), F32)],
    )
    (result,) = call(
        result_kernel,
        "result",
        [shape((local_rows, local_features), BF16)],
        [],
        [keep] + [swap(low, "req", m + 1) for m, low in enumerate(lows)],
    )
    return (result, new_state, new_entries)


def solution(mesh):
    return jax.shard_map(
        per_device,
        mesh=mesh,
        in_specs=(
            P(("grp", "req"), "chan"),
            P("chan"),
            P(None, "chan", "req"),
            P(None, "req"),
            P("req"),
            P(None, ("grp", "chan"), "req"),
            P(None, "req", None, None),
            P(None, "req"),
            P("req"),
            P(("grp", "chan"), "req"),
            P("req", "chan"),
            P("chan"),
            P("chan", "req"),
            P("chan", None),
            P(("grp", "req", "chan"), None, None),
            P(("grp", "req", "chan"), None, None),
            P(("grp", "req", "chan")),
            P(("grp", "req", "chan")),
            P("req", "chan"),
            P("chan"),
            P(None, "chan", "req"),
            P("req", "chan"),
        ),
        out_specs=(
            P(("grp", "req"), "chan"),
            P(("grp", "chan"), "req"),
            P(("grp", "req", "chan"), None),
        ),
        check_vma=False,
    )
```
